1024 devices in a mesh: fsdp: 8 (over x, core), tensor: 128 (over z, y).
Axes of the slice: x: 4, y: 4, z: 32, core: 2. Of those that a mesh axis runs over, the one named last changes fastest.
Arguments:
- weight: bfloat16 [14336, 4096], P('tensor', 'fsdp'), may hold values from -0.0017929077 to 0.0017929077
- momentum: float32 [14336, 4096], P('tensor', 'fsdp'), may hold values from -18 to 18
- grad: bfloat16 [14336, 4096], P('tensor', 'fsdp'), may hold values from -6 to 6
- q_prev: float32 [14336, 256], P('tensor'), may hold values from -0.046875 to 0.046875
Outputs:
- new_weight: bfloat16 [14336, 4096], P('tensor', 'fsdp')
- new_momentum: float32 [14336, 4096], P('tensor', 'fsdp')
- q_new: float32 [14336, 256], P('tensor')
The draws below stay inside these ranges and needn't reach their ends.
All inputs are finite; a program needn't handle non-finite values.
Results may differ from the reference program's by a relative error of at most 0.001.
Values sent between devices are 32-bit elements; how exact they have to be, the bound alone decides.
A program may use at most 32 MiB of HBM per device.

```python
import math
import jax
import jax.numpy as jnp
from jax import lax

RANK = 256
D = 4096
FF = 14336


def draw_momentum(key, part):
    position = jnp.arange(FF, dtype=jnp.float32)[:, None] / FF
    base = jnp.clip(jax.random.normal(key, (FF, D), jnp.float32), -6.0, 6.0)
    scale = jnp.exp(position * jnp.log(3.0))
    return base * scale


def level_of(rng, extent, cuts, low, top_value):
    def one(dim, parts):
        draws = jax.random.uniform(jax.random.fold_in(jax.random.fold_in(rng, 6), dim), (parts,), jnp.float32, low / len(cuts), top_value / len(cuts))
        return jnp.repeat(jnp.exp(draws), extent[dim] // parts).reshape((-1,) + (1,) * (len(extent) - dim - 1))

    gain = one(*cuts[0])
    for cut in cuts[1:]:
        gain = gain * one(*cut)
    return gain


def normal_values(key, dims, width, most, shards=(), held_as=jnp.bfloat16):
    entries = jax.random.normal(key, dims, jnp.float32) * width
    if len(shards) > 0:
        entries = level_of(key, dims, shards, -0.22, 0.18) * entries
    return jnp.clip(entries, min=-most, max=most).astype(held_as)


def setup_inputs(seed: int = 0) -> dict:
    seeds = jax.random.split(jax.random.key(seed), 5)
    weight = normal_values(seeds[0], (FF, D), 0.0003, 0.0017929077, ((0, 128), (1, 8)))
    momentum = draw_momentum(jax.random.fold_in(seeds[4], 71), 0)
    grad = normal_values(seeds[2], (FF, D), 1.0, 6.0, ((0, 128), (1, 8)))
    q_prev = normal_values(seeds[3], (FF, RANK), FF ** -0.5, 0.046875, ((0, 128),), jnp.float32)
    return {"weight": weight, "momentum": momentum, "grad": grad, "q_prev": q_prev}


momentum_decay = 0.95
step_rate = 0.02
norm_eps = 1e-06

def reference(weight, momentum, grad, q_prev):
    highest = lax.Precision.HIGHEST
    buffer = momentum + grad.astype(jnp.float32)
    power = lax.dot_general(buffer.astype(jnp.float32), q_prev.astype(jnp.float32), (((0,), (0,)), ((), ())), precision=highest, preferred_element_type=jnp.float32)
    gram = lax.dot_general(power.astype(jnp.float32), power.astype(jnp.float32), (((0,), (0,)), ((), ())), precision=highest, preferred_element_type=jnp.float32)
    lower = jnp.linalg.cholesky(gram)
    ortho = jax.scipy.linalg.solve_triangular(lower, power.T, lower=True).T
    right = jnp.dot(buffer.astype(jnp.float32), ortho.astype(jnp.float32), precision=highest, preferred_element_type=jnp.float32)
    colnorm = jnp.sqrt(lax.optimization_barrier(jnp.sum(right * right, axis=0)))
    q_new = right / (colnorm + norm_eps)
    new_momentum = buffer - (1.0 - momentum_decay) * jnp.dot(right.astype(jnp.float32), ortho.T.astype(jnp.float32), precision=highest, preferred_element_type=jnp.float32)
    factor = step_rate * math.sqrt(FF / D)
    update = jnp.dot(q_new.astype(jnp.float32), ortho.T.astype(jnp.float32), precision=highest, preferred_element_type=jnp.float32)
    new_weight = (weight.astype(jnp.float32) - factor * update).astype(jnp.bfloat16)
    return (new_weight, new_momentum, q_new)
```

```python
import functools
import math

import jax
import jax.numpy as jnp
from jax import lax
from jax.experimental import pallas as pl
from jax.experimental.pallas import tpu as pltpu
from jax.sharding import Mesh
from jax.sharding import PartitionSpec as P

TENSOR = ("zf", "zn", "y")
MESH_ID = pl.DeviceIdType.MESH
TILES = 128
GRAM_TILES = 48
CROSS_TILES = 32

momentum_decay = 0.95
step_rate = 0.02
norm_eps = 1e-06


def dot(left, right, dims):
    return lax.dot_general(
        left,
        right,
        (dims, ((), ())),
        precision=lax.Precision.HIGHEST,
        preferred_element_type=jnp.float32,
    )


def far_first(n):
    return sorted(range(1, n), key=lambda d: -min(d, n - d)) + [0]


def remote(src, dst, send, recv, device):
    copy = pltpu.make_async_remote_copy(
        src_ref=src,
        dst_ref=dst,
        send_sem=send,
        recv_sem=recv,
        device_id=device,
        device_id_type=MESH_ID,
    )
    copy.start()


def drain(ref, sem):
    pltpu.make_async_copy(ref, ref, sem).wait()


def greet(axes):
    barrier = pltpu.get_barrier_semaphore()
    count = 0
    for axis, n in axes:
        me = lax.axis_index(axis)
        for d in range(1, n):
            pl.semaphore_signal(
                barrier, inc=1, device_id={axis: (me + d) % n}, device_id_type=MESH_ID
            )
            count += 1
    pl.semaphore_wait(barrier, count)


def sum_over(axis, n, part, got, total, per, sems):
    me = lax.axis_index(axis)

    def scatter():
        for d in range(1, n):
            k = (me + d) % n
            remote(part.at[pl.ds(k * per, per)], got.at[d - 1], sems.at[0], sems.at[1], {axis: k})

    def gather():
        drain(got, sems.at[1])
        mine = part[pl.ds(me * per, per)]
        for d in range(1, n):
            mine = mine + got[d - 1]
        own = total.at[pl.ds(me * per, per)]
        own[...] = mine
        for d in range(1, n):
            remote(own, own, sems.at[2], sems.at[3], {axis: (me + d) % n})

    def finish():
        drain(got, sems.at[0])
        drain(got, sems.at[2])
        drain(got, sems.at[3])

    return scatter, gather, finish


def power_kernel(
    sizes,
    momentum_ref,
    grad_ref,
    q_ref,
    power_ref,
    gram_ref,
    cross_ref,
    part,
    full,
    got_y,
    got_n,
    got_f,
    sum_y,
    sum_n,
    gram_part,
    gram_got,
    gram_total,
    cross_part,
    cross_got,
    cross_total,
    rs_send,
    rs_y,
    rs_n,
    rs_f,
    ag_send,
    ag_y,
    ag_n,
    ag_f,
    gram_sem,
    cross_sem,
):
    n_fsdp, n_f, n_n, n_y = sizes
    unit = TILES // (n_f * n_n * n_y)
    f_me, n_me, y_me = lax.axis_index("zf"), lax.axis_index("zn"), lax.axis_index("y")
    order = far_first(n_f)

    def chunk(f, y):
        return pl.ds((f * n_y + y) * (n_n * unit), n_n * unit)

    def tile(f, n, y):
        return pl.ds(((f * n_y + y) * n_n + n) * unit, unit)

    buffer = momentum_ref[...] + grad_ref[...].astype(jnp.float32)
    local = dot(buffer, q_ref[...], ((0,), (0,)))
    half = TILES // 2
    part[0:half] = local[:, 0:128].reshape(half, 8, 128)
    part[half:TILES] = local[:, 128:256].reshape(half, 8, 128)
    greet((("y", n_y), ("zn", n_n), ("zf", n_f), ("fsdp", n_fsdp)))

    for i, d in enumerate(order):
        f = (f_me + d) % n_f
        for e in range(1, n_y):
            y = (y_me + e) % n_y
            remote(part.at[chunk(f, y)], got_y.at[i, e - 1], rs_send.at[0], rs_y.at[i], {"y": y})

    def after_y(i):
        drain(got_y.at[i], rs_y.at[i])
        total = part[chunk((f_me + order[i]) % n_f, y_me)]
        for e in range(1, n_y):
            total = total + got_y[i, e - 1]
        sum_y[i] = total
        for e in range(1, n_n):
            n = (n_me + e) % n_n
            remote(
                sum_y.at[i, pl.ds(n * unit, unit)], got_n.at[i, e - 1], rs_send.at[1], rs_n.at[i], {"zn": n}
            )

    def after_n(i):
        drain(got_n.at[i], rs_n.at[i])
        total = sum_y[i, pl.ds(n_me * unit, unit)]
        for e in range(1, n_n):
            total = total + got_n[i, e - 1]
        sum_n[i] = total
        d = order[i]
        if d:
            remote(sum_n.at[i], got_f.at[d - 1], rs_send.at[2], rs_f, {"zf": (f_me + d) % n_f})

    lag = n_f // 2
    for i in range(n_f + lag):
        if i < n_f:
            after_y(i)
        if i >= lag:
            after_n(i - lag)
    drain(got_f, rs_f)
    total = sum_n[n_f - 1]
    for d in range(1, n_f):
        total = total + got_f[d - 1]

    own = full.at[tile(f_me, n_me, y_me)]
    own[...] = total
    for d in order[:-1]:
        remote(own, own, ag_send.at[0], ag_f.at[d], {"zf": (f_me + d) % n_f})

    def spread_n(d):
        f = (f_me - d + n_f) % n_f
        mine = full.at[tile(f, n_me, y_me)]
        if d:
            drain(mine, ag_f.at[d])
        for e in range(1, n_n):
            remote(mine, mine, ag_send.at[1], ag_n.at[d], {"zn": (n_me + e) % n_n})

    def spread_y(d):
        drain(full.at[0 : (n_n - 1) * unit], ag_n.at[d])
        mine = full.at[chunk((f_me - d + n_f) % n_f, y_me)]
        for e in range(1, n_y):
            remote(mine, mine, ag_send.at[2], ag_y, {"y": (y_me + e) % n_y})

    near = order[::-1]
    for i in range(n_f + 1):
        if i < n_f:
            spread_n(near[i])
        if i >= 1:
            spread_y(near[i - 1])
    drain(full.at[0 : TILES // n_y * (n_y - 1)], ag_y)

    left = full[0:half].reshape(half * 8, 128)
    right = full[half:TILES].reshape(half * 8, 128)
    whole = jnp.concatenate([left, right], axis=1)
    gram = dot(whole, whole, ((0,), (0,)))
    for i, (r, c) in enumerate(((0, 0), (0, 1), (1, 1))):
        block = gram[r * 128 : (r + 1) * 128, c * 128 : (c + 1) * 128]
        gram_part[i * 16 : (i + 1) * 16] = block.reshape(16, 8, 128)
    gram_scatter, gram_gather, gram_finish = sum_over(
        "fsdp", n_fsdp, gram_part, gram_got, gram_total, GRAM_TILES // n_fsdp, gram_sem
    )
    cross_scatter, cross_gather, cross_finish = sum_over(
        "fsdp", n_fsdp, cross_part, cross_got, cross_total, CROSS_TILES // n_fsdp, cross_sem
    )
    gram_scatter()
    cross = dot(buffer, whole, ((1,), (0,)))
    cross_part[0:14] = cross[:, 0:128].reshape(14, 8, 128)
    cross_part[14:28] = cross[:, 128:256].reshape(14, 8, 128)
    cross_part[28:32] = jnp.zeros((4, 8, 128), jnp.float32)
    cross_scatter()
    gram_gather()
    cross_gather()
    gram_finish()
    cross_finish()
    sent_y = TILES // n_y * (n_y - 1)
    drain(part.at[0:sent_y], rs_send.at[0])
    drain(got_n, rs_send.at[1])
    drain(got_f, rs_send.at[2])
    drain(got_f, ag_send.at[0])
    drain(got_n, ag_send.at[1])
    drain(part.at[0:sent_y], ag_send.at[2])
    power_ref[...] = full[...]
    gram_ref[...] = gram_total[...]
    cross_ref[...] = cross_total[...]


def eliminate(m):
    sub = lax.broadcasted_iota(jnp.int32, (8, 128), 0)
    lane = lax.broadcasted_iota(jnp.int32, (8, 128), 1)
    for p in range(16):
        lo, hi = 8 * p, 8 * p + 8
        rows = [m[lo:hi, 128 * c : 128 * (c + 1)] for c in range(3)]
        cols = [jnp.broadcast_to(rows[0][:, lo + j : lo + j + 1], (8, 128)) for j in range(8)]
        for j in range(8):
            scale = lax.rsqrt(cols[j][j : j + 1, :])
            factor = cols[j] * scale
            for k in range(j + 1, 8):
                cols[k] = cols[k] - factor * factor[k : k + 1, :]
            below = jnp.where(sub > j, factor, 0.0)
            for c in range(3):
                top = rows[c][j : j + 1, :] * scale
                rows[c] = jnp.where(sub == j, top, rows[c] - below * top)
        for c in range(3):
            m[lo:hi, 128 * c : 128 * (c + 1)] = rows[c]
        if p < 15:
            above = jnp.where(lane >= hi, rows[0], 0.0)
            change = dot(above, jnp.concatenate(rows, axis=1), ((0,), (0,)))
            m[hi:128, :] = m[hi:128, :] - change[hi:128, :]


def factor_kernel(
    power_ref, gram_ref, cross_ref, momentum_ref, grad_ref, right_ref, ortho_ref, square_ref, new_momentum_ref, m
):
    eye = (
        lax.broadcasted_iota(jnp.int32, (128, 128), 0) == lax.broadcasted_iota(jnp.int32, (128, 128), 1)
    ).astype(jnp.float32)
    m[:, 0:128] = gram_ref[0:16].reshape(128, 128)
    m[:, 128:256] = gram_ref[16:32].reshape(128, 128)
    m[:, 256:384] = eye
    eliminate(m)
    across, first = m[:, 128:256], m[:, 256:384]
    m[:, 0:128] = gram_ref[32:48].reshape(128, 128) - dot(across, across, ((0,), (0,)))
    m[:, 128:256] = -dot(across, first, ((0,), (0,)))
    m[:, 256:384] = eye
    eliminate(m)
    inverse = jnp.concatenate(
        [jnp.concatenate([first, jnp.zeros_like(first)], axis=1), m[:, 128:384]], axis=0
    )
    cross = jnp.concatenate([cross_ref[0:14].reshape(112, 128), cross_ref[14:28].reshape(112, 128)], axis=1)
    right = dot(cross, inverse, ((1,), (1,)))
    right_ref[...] = right
    square_ref[...] = jnp.sum(right * right, axis=0, keepdims=True)
    half = TILES // 2
    power = jnp.concatenate(
        [power_ref[0:half].reshape(half * 8, 128), power_ref[half:TILES].reshape(half * 8, 128)], axis=1
    )
    ortho = dot(power, inverse, ((1,), (1,)))
    ortho_ref[...] = ortho
    buffer = momentum_ref[...] + grad_ref[...].astype(jnp.float32)
    new_momentum_ref[...] = buffer - (1.0 - momentum_decay) * dot(right, ortho, ((1,), (1,)))


def norm_kernel(sizes, square_ref, out_ref, total, got_y, got_n, got_f, send, recv):
    axes = (("y", sizes[3]), ("zn", sizes[2]), ("zf", sizes[1]))
    greet(axes)
    value = square_ref[...]
    for i, ((axis, n), got) in enumerate(zip(axes, (got_y, got_n, got_f))):
        me = lax.axis_index(axis)
        total[i] = value
        for d in far_first(n)[:-1]:
            remote(total.at[i], got.at[d - 1], send.at[i], recv.at[i], {axis: (me + d) % n})
        drain(got, recv.at[i])
        for d in range(1, n):
            value = value + got[d - 1]
    for i, got in enumerate((got_y, got_n, got_f)):
        drain(got, send.at[i])
    out_ref[...] = value


def final_kernel(factor, weight_ref, right_ref, ortho_ref, square_ref, new_weight_ref, q_ref):
    q = right_ref[...] / (jnp.sqrt(square_ref[...]) + norm_eps)
    q_ref[...] = q
    update = dot(q, ortho_ref[...], ((1,), (1,)))
    new_weight_ref[...] = (weight_ref[...].astype(jnp.float32) - factor * update).astype(jnp.bfloat16)


def per_device(sizes, factor, weight, momentum, grad, q_prev):
    n_fsdp, n_f, n_n, n_y = sizes
    unit = TILES // (n_f * n_n * n_y)
    f32 = jnp.float32
    vmem = pl.BlockSpec(memory_space=pltpu.VMEM)

    def like(*shape):
        return jax.ShapeDtypeStruct(shape, f32)

    def tiles(*shape):
        return pltpu.VMEM((*shape, 8, 128), f32)

    dma = pltpu.SemaphoreType.DMA
    gram_per, cross_per = GRAM_TILES // n_fsdp, CROSS_TILES // n_fsdp
    power, gram, cross = pl.pallas_call(
        functools.partial(power_kernel, sizes),
        out_shape=(like(TILES, 8, 128), like(GRAM_TILES, 8, 128), like(CROSS_TILES, 8, 128)),
        in_specs=[vmem] * 3,
        out_specs=(vmem,) * 3,
        scratch_shapes=[
            tiles(TILES),
            tiles(TILES),
            tiles(n_f, n_y - 1, n_n * unit),
            tiles(n_f, n_n - 1, unit),
            tiles(n_f - 1, unit),
            tiles(n_f, n_n * unit),
            tiles(n_f, unit),
            tiles(GRAM_TILES),
            tiles(n_fsdp - 1, gram_per),
            tiles(GRAM_TILES),
            tiles(CROSS_TILES),
            tiles(n_fsdp - 1, cross_per),
            tiles(CROSS_TILES),
            dma((3,)),
            dma((n_f,)),
            dma((n_f,)),
            dma,
            dma((3,)),
            dma,
            dma((n_f,)),
            dma((n_f,)),
            dma((4,)),
            dma((4,)),
        ],
        compiler_params=pltpu.CompilerParams(collective_id=0, has_side_effects=True),
        name="power",
    )(momentum, grad, q_prev)
    rows, cols = momentum.shape
    right, ortho, square, new_momentum = pl.pallas_call(
        factor_kernel,
        out_shape=(like(rows, 256), like(cols, 256), like(1, 256), like(rows, cols)),
        in_specs=[vmem] * 5,
        out_specs=(vmem,) * 4,
        scratch_shapes=[pltpu.VMEM((128, 384), f32)],
        name="factor",
    )(power, gram, cross, momentum, grad)
    square = pl.pallas_call(
        functools.partial(norm_kernel, sizes),
        out_shape=like(1, 256),
        in_specs=[vmem],
        out_specs=vmem,
        scratch_shapes=[
            pltpu.VMEM((3, 1, 256), f32),
            pltpu.VMEM((n_y - 1, 1, 256), f32),
            pltpu.VMEM((n_n - 1, 1, 256), f32),
            pltpu.VMEM((n_f - 1, 1, 256), f32),
            dma((3,)),
            dma((3,)),
        ],
        compiler_params=pltpu.CompilerParams(collective_id=1, has_side_effects=True),
        name="norm",
    )(square)
    new_weight, q_new = pl.pallas_call(
        functools.partial(final_kernel, factor),
        out_shape=(jax.ShapeDtypeStruct((rows, cols), jnp.bfloat16), like(rows, 256)),
        in_specs=[vmem] * 4,
        out_specs=(vmem,) * 2,
        name="final",
    )(weight, right, ortho, square)
    return new_weight, new_momentum, q_new


def split_tensor(n):
    return (8, 4, 4) if n == 128 else (n // 4, 2, 2)


def solution(mesh):
    n_fsdp, n_tensor = mesh.shape["fsdp"], mesh.shape["tensor"]
    sizes = (n_fsdp, *split_tensor(n_tensor))
    torus = Mesh(mesh.devices.reshape(sizes), ("fsdp", *TENSOR))
    factor = step_rate * math.sqrt(14336 / 4096)
    return jax.shard_map(
        functools.partial(per_device, sizes, factor),
        mesh=torus,
        in_specs=(P(TENSOR, "fsdp"), P(TENSOR, "fsdp"), P(TENSOR, "fsdp"), P(TENSOR, None)),
        out_specs=(P(TENSOR, "fsdp"), P(TENSOR, "fsdp"), P(TENSOR, None)),
        check_vma=False,
    )
```

```python
import functools
import math

import jax
import jax.numpy as jnp
from jax import lax
from jax.experimental import pallas as pl
from jax.experimental.pallas import tpu as pltpu
from jax.sharding import Mesh
from jax.sharding import PartitionSpec as P

TENSOR = ("zf", "zn", "y")
MESH_ID = pl.DeviceIdType.MESH
TILES = 128
GRAM_TILES = 48
CROSS_TILES = 32
PANEL = 32

momentum_decay = 0.95
step_rate = 0.02
norm_eps = 1e-06


def dot(left, right, dims):
    return lax.dot_general(
        left,
        right,
        (dims, ((), ())),
        precision=lax.Precision.HIGHEST,
        preferred_element_type=jnp.float32,
    )


def far_first(n):
    return sorted(range(1, n), key=lambda d: -min(d, n - d)) + [0]


def remote(src, dst, send, recv, device):
    copy = pltpu.make_async_remote_copy(
        src_ref=src,
        dst_ref=dst,
        send_sem=send,
        recv_sem=recv,
        device_id=device,
        device_id_type=MESH_ID,
    )
    copy.start()


def drain(ref, sem):
    pltpu.make_async_copy(ref, ref, sem).wait()


def greet(peers):
    barrier = pltpu.get_barrier_semaphore()
    for peer in peers:
        pl.semaphore_signal(barrier, inc=1, device_id=peer, device_id_type=MESH_ID)
    pl.semaphore_wait(barrier, len(peers))


def others(axis, n, steps=None):
    me = lax.axis_index(axis)
    return [{axis: (me + d) % n} for d in (range(1, n) if steps is None else steps)]


def sum_over(axis, n, part, got, total, per, sems):
    me = lax.axis_index(axis)

    def scatter():
        for d in range(1, n):
            k = (me + d) % n
            remote(part.at[pl.ds(k * per, per)], got.at[d - 1], sems.at[0], sems.at[1], {axis: k})

    def gather():
        drain(got, sems.at[1])
        mine = part[pl.ds(me * per, per)]
        for d in range(1, n):
            mine = mine + got[d - 1]
        own = total.at[pl.ds(me * per, per)]
        own[...] = mine
        for d in range(1, n):
            remote(own, own, sems.at[2], sems.at[3], {axis: (me + d) % n})

    def finish():
        drain(got, sems.at[0])
        drain(got, sems.at[2])
        drain(got, sems.at[3])

    return scatter, gather, finish


def eliminate(m):
    sub = lax.broadcasted_iota(jnp.int32, (8, 128), 0)
    lane = lax.broadcasted_iota(jnp.int32, (PANEL, 128), 1)
    groups = PANEL // 8

    def panel(p, carry):
        lo = pl.multiple_of(p * PANEL, PANEL)
        block = pltpu.roll(m[pl.ds(lo, PANEL), 0:128], (128 - lo) % 128, axis=1)
        rows = [
            [m[pl.ds(lo + 8 * v, 8), 128 * c : 128 * (c + 1)] for c in range(3)] for v in range(groups)
        ]
        cols = [
            {v: jnp.broadcast_to(block[8 * v : 8 * v + 8, j : j + 1], (8, 128)) for v in range(j // 8, groups)}
            for j in range(PANEL)
        ]
        for j in range(PANEL):
            top_group, s = j // 8, j % 8
            scale = lax.rsqrt(cols[j][top_group][s : s + 1, :])
            factor = {v: cols[j][v] * scale for v in range(top_group, groups)}
            for k in range(j + 1, PANEL):
                mult = factor[k // 8][k % 8 : k % 8 + 1, :]
                for v in range(k // 8, groups):
                    cols[k][v] = cols[k][v] - factor[v] * mult
            below = jnp.where(sub > s, factor[top_group], 0.0)
            for c in range(3):
                top = rows[top_group][c][s : s + 1, :] * scale
                rows[top_group][c] = jnp.where(sub == s, top, rows[top_group][c] - below * top)
                for v in range(top_group + 1, groups):
                    rows[v][c] = rows[v][c] - factor[v] * top
        done = jnp.concatenate([jnp.concatenate(row, axis=1) for row in rows], axis=0)
        m[pl.ds(lo, PANEL), :] = done
        above = jnp.where(lane >= lo + PANEL, done[:, 0:128], 0.0)
        m[...] = m[...] - dot(above, done, ((0,), (0,)))
        return carry

    lax.fori_loop(0, 128 // PANEL, panel, 0)


def step_kernel(
    sizes,
    factor,
    weight_ref,
    momentum_ref,
    grad_ref,
    q_ref,
    new_weight_ref,
    new_momentum_ref,
    new_q_ref,
    part,
    full,
    got_y,
    got_n,
    sum_y,
    sum_n,
    ring_left,
    ring_right,
    out_left,
    out_right,
    gram_part,
    gram_got,
    gram_total,
    cross_part,
    cross_got,
    cross_total,
    m,
    square,
    square_y,
    square_z,
    rs_send,
    rs_y,
    rs_n,
    rs_left,
    rs_right,
    ag_send,
    ag_y,
    ag_n,
    ag_f,
    gram_sem,
    cross_sem,
    square_sem,
):
    n_fsdp, n_f, n_n, n_y = sizes
    unit = TILES // (n_f * n_n * n_y)
    f_me, n_me, y_me = lax.axis_index("zf"), lax.axis_index("zn"), lax.axis_index("y")
    order = far_first(n_f)
    far = n_f // 2
    half = TILES // 2

    def chunk(f, y):
        return pl.ds((f * n_y + y) * (n_n * unit), n_n * unit)

    def tile(f, n, y):
        return pl.ds(((f * n_y + y) * n_n + n) * unit, unit)

    buffer = momentum_ref[...] + grad_ref[...].astype(jnp.float32)
    local = dot(buffer, q_ref[...], ((0,), (0,)))
    part[0:half] = local[:, 0:128].reshape(half, 8, 128)
    part[half:TILES] = local[:, 128:256].reshape(half, 8, 128)
    greet(
        others("y", n_y)
        + others("zn", n_n)
        + others("zf", n_f, sorted({1, n_f - 1}))
        + others("fsdp", n_fsdp)
    )

    for i, d in enumerate(order):
        f = (f_me + d) % n_f
        for e in range(1, n_y):
            y = (y_me + e) % n_y
            remote(part.at[chunk(f, y)], got_y.at[i, e - 1], rs_send.at[0], rs_y.at[i], {"y": y})

    def after_y(i):
        drain(got_y.at[i], rs_y.at[i])
        total = part[chunk((f_me + order[i]) % n_f, y_me)]
        for e in range(1, n_y):
            total = total + got_y[i, e - 1]
        sum_y[i] = total
        for e in range(1, n_n):
            n = (n_me + e) % n_n
            remote(
                sum_y.at[i, pl.ds(n * unit, unit)], got_n.at[i, e - 1], rs_send.at[1], rs_n.at[i], {"zn": n}
            )

    left = ((f_me + n_f - 1) % n_f, ring_left, out_left, rs_left, rs_send.at[2], far, lambda s: far + s)
    right = (
        (f_me + 1) % n_f,
        ring_right,
        out_right,
        rs_right,
        rs_send.at[3],
        n_f - 1 - far,
        lambda s: n_f - 1 - far - s,
    )

    def ring_step(way, s):
        peer, ring, out, recv, send, length, piece = way
        if s < length:
            value = sum_n[order.index(piece(s))]
            if s:
                drain(ring.at[s - 1], recv.at[s - 1])
                value = value + ring[s - 1]
            out[s] = value
            remote(out.at[s], ring.at[s], send, recv.at[s], {"zf": peer})

    def after_n(i):
        drain(got_n.at[i], rs_n.at[i])
        total = sum_y[i, pl.ds(n_me * unit, unit)]
        for e in range(1, n_n):
            total = total + got_n[i, e - 1]
        sum_n[i] = total
        for way in (left, right):
            if way[5] and order[i] == way[6](0):
                ring_step(way, 0)

    lag = n_f // 2
    for i in range(n_f + lag):
        if i < n_f:
            after_y(i)
        if i >= lag:
            after_n(i - lag)
    for s in range(1, far):
        ring_step(left, s)
        ring_step(right, s)
    total = sum_n[n_f - 1]
    for peer, ring, out, recv, send, length, piece in (left, right):
        if length:
            drain(ring.at[length - 1], recv.at[length - 1])
            total = total + ring[length - 1]

    own = full.at[tile(f_me, n_me, y_me)]
    own[...] = total
    for n in range(n_n):
        peer = {"zf": (f_me + far) % n_f, "zn": (n_me + n) % n_n}
        remote(own, own, ag_send.at[0], ag_f.at[far], peer)
    for d in order[1:-1]:
        remote(own, own, ag_send.at[0], ag_f.at[d], {"zf": (f_me + d) % n_f})

    def spread_n(d):
        mine = full.at[tile((f_me - d + n_f) % n_f, n_me, y_me)]
        if d:
            drain(mine, ag_f.at[d])
        for e in range(1, n_n):
            remote(mine, mine, ag_send.at[1], ag_n.at[d], {"zn": (n_me + e) % n_n})

    def spread_y(d):
        mine = full.at[chunk((f_me - d + n_f) % n_f, y_me)]
        if d == far:
            drain(mine, ag_f.at[d])
        else:
            drain(full.at[0 : (n_n - 1) * unit], ag_n.at[d])
        for e in range(1, n_y):
            remote(mine, mine, ag_send.at[2], ag_y, {"y": (y_me + e) % n_y})

    near = order[:0:-1]
    lag = min(3, n_f - 1)
    for i in range(n_f - 1 + lag):
        if i < n_f - 1:
            spread_n(near[i])
        if i == n_f:
            spread_y(far)
        if i >= lag:
            spread_y(near[i - lag])
    if n_f - 1 + lag <= n_f:
        spread_y(far)
    drain(full.at[0 : TILES // n_y * (n_y - 1)], ag_y)

    whole = jnp.concatenate(
        [full[0:half].reshape(half * 8, 128), full[half:TILES].reshape(half * 8, 128)], axis=1
    )
    gram = dot(whole, whole, ((0,), (0,)))
    for i, (r, c) in enumerate(((0, 0), (0, 1), (1, 1))):
        block = gram[r * 128 : (r + 1) * 128, c * 128 : (c + 1) * 128]
        gram_part[i * 16 : (i + 1) * 16] = block.reshape(16, 8, 128)
    gram_scatter, gram_gather, gram_finish = sum_over(
        "fsdp", n_fsdp, gram_part, gram_got, gram_total, GRAM_TILES // n_fsdp, gram_sem
    )
    cross_scatter, cross_gather, cross_finish = sum_over(
        "fsdp", n_fsdp, cross_part, cross_got, cross_total, CROSS_TILES // n_fsdp, cross_sem
    )
    gram_scatter()
    cross = dot(buffer, whole, ((1,), (0,)))
    cross_part[0:14] = cross[:, 0:128].reshape(14, 8, 128)
    cross_part[14:28] = cross[:, 128:256].reshape(14, 8, 128)
    cross_part[28:32] = jnp.zeros((4, 8, 128), jnp.float32)
    gram_gather()
    cross_scatter()
    gram_finish()

    eye = (
        lax.broadcasted_iota(jnp.int32, (128, 128), 0) == lax.broadcasted_iota(jnp.int32, (128, 128), 1)
    ).astype(jnp.float32)
    m[:, 0:128] = gram_total[0:16].reshape(128, 128)
    m[:, 128:256] = gram_total[16:32].reshape(128, 128)
    m[:, 256:384] = eye
    eliminate(m)
    cross_gather()
    across, first = m[:, 128:256], m[:, 256:384]
    m[:, 0:128] = gram_total[32:48].reshape(128, 128) - dot(across, across, ((0,), (0,)))
    m[:, 128:256] = -dot(across, first, ((0,), (0,)))
    m[:, 256:384] = eye
    eliminate(m)
    inverse = jnp.concatenate(
        [jnp.concatenate([first, jnp.zeros_like(first)], axis=1), m[:, 128:384]], axis=0
    )
    cross_finish()
    cross = jnp.concatenate(
        [cross_total[0:14].reshape(112, 128), cross_total[14:28].reshape(112, 128)], axis=1
    )
    right_factor = dot(cross, inverse, ((1,), (1,)))

    value = jnp.sum(right_factor * right_factor, axis=0, keepdims=True)
    square[0] = value
    for d in range(1, n_y):
        remote(square.at[0], square_y.at[d - 1], square_sem.at[0], square_sem.at[1], {"y": (y_me + d) % n_y})
    ortho = dot(whole, inverse, ((1,), (1,)))
    drain(square_y, square_sem.at[1])
    for d in range(1, n_y):
        value = value + square_y[d - 1]
    square[1] = value
    n_z = n_f * n_n
    z_me = f_me * n_n + n_me
    for d in far_first(n_z)[:-1]:
        z = (z_me + d) % n_z
        peer = {"zf": z // n_n, "zn": z % n_n}
        remote(square.at[1], square_z.at[d - 1], square_sem.at[2], square_sem.at[3], peer)
    new_momentum_ref[...] = buffer - (1.0 - momentum_decay) * dot(right_factor, ortho, ((1,), (1,)))

    drain(part.at[0 : TILES // n_y * (n_y - 1)], rs_send.at[0])
    drain(got_n, rs_send.at[1])
    for peer, ring, out, recv, send, length, piece in (left, right):
        if length:
            drain(out.at[0:length], send)
    drain(full.at[0 : (n_f - 2 + n_n) * unit], ag_send.at[0])
    drain(full.at[0 : (n_f - 1) * (n_n - 1) * unit], ag_send.at[1])
    drain(full.at[0 : TILES // n_y * (n_y - 1)], ag_send.at[2])
    drain(square_y, square_sem.at[0])
    drain(square_z, square_sem.at[3])
    drain(square_z, square_sem.at[2])
    for d in range(1, n_z):
        value = value + square_z[d - 1]
    q_new = right_factor / (jnp.sqrt(value) + norm_eps)
    new_q_ref[...] = q_new
    update = dot(q_new, ortho, ((1,), (1,)))
    new_weight_ref[...] = (weight_ref[...].astype(jnp.float32) - factor * update).astype(jnp.bfloat16)


def per_device(sizes, factor, weight, momentum, grad, q_prev):
    n_fsdp, n_f, n_n, n_y = sizes
    unit = TILES // (n_f * n_n * n_y)
    far = n_f // 2
    vmem = pl.BlockSpec(memory_space=pltpu.VMEM)
    dma = pltpu.SemaphoreType.DMA

    def tiles(*shape):
        return pltpu.VMEM((*shape, 8, 128), jnp.float32)

    def row(*shape):
        return pltpu.VMEM((*shape, 1, 256), jnp.float32)

    gram_per, cross_per = GRAM_TILES // n_fsdp, CROSS_TILES // n_fsdp
    return pl.pallas_call(
        functools.partial(step_kernel, sizes, factor),
        out_shape=(
            jax.ShapeDtypeStruct(weight.shape, jnp.bfloat16),
            jax.ShapeDtypeStruct(momentum.shape, jnp.float32),
            jax.ShapeDtypeStruct(q_prev.shape, jnp.float32),
        ),
        in_specs=[vmem] * 4,
        out_specs=(vmem,) * 3,
        scratch_shapes=[
            tiles(TILES),
            tiles(TILES),
            tiles(n_f, n_y - 1, n_n * unit),
            tiles(n_f, n_n - 1, unit),
            tiles(n_f, n_n * unit),
            tiles(n_f, unit),
            tiles(far, unit),
            tiles(far, unit),
            tiles(far, unit),
            tiles(far, unit),
            tiles(GRAM_TILES),
            tiles(n_fsdp - 1, gram_per),
            tiles(GRAM_TILES),
            tiles(CROSS_TILES),
            tiles(n_fsdp - 1, cross_per),
            tiles(CROSS_TILES),
            pltpu.VMEM((128, 384), jnp.float32),
            row(2),
            row(n_y - 1),
            row(n_f * n_n - 1),
            dma((4,)),
            dma((n_f,)),
            dma((n_f,)),
            dma((far,)),
            dma((far,)),
            dma((3,)),
            dma,
            dma((n_f,)),
            dma((n_f,)),
            dma((4,)),
            dma((4,)),
            dma((4,)),
        ],
        compiler_params=pltpu.CompilerParams(collective_id=0, has_side_effects=True),
        name="step",
    )(weight, momentum, grad, q_prev)


def split_tensor(n):
    return (8, 4, 4) if n == 128 else (n // 4, 2, 2)


def solution(mesh):
    n_fsdp, n_tensor = mesh.shape["fsdp"], mesh.shape["tensor"]
    sizes = (n_fsdp, *split_tensor(n_tensor))
    torus = Mesh(mesh.devices.reshape(sizes), ("fsdp", *TENSOR))
    factor = step_rate * math.sqrt(14336 / 4096)
    return jax.shard_map(
        functools.partial(per_device, sizes, factor),
        mesh=torus,
        in_specs=(P(TENSOR, "fsdp"), P(TENSOR, "fsdp"), P(TENSOR, "fsdp"), P(TENSOR, None)),
        out_specs=(P(TENSOR, "fsdp"), P(TENSOR, "fsdp"), P(TENSOR, None)),
        check_vma=False,
    )
```

```python
import functools
import math

import jax
import jax.numpy as jnp
from jax import lax
from jax.experimental import pallas as pl
from jax.experimental.pallas import tpu as pltpu
from jax.sharding import Mesh
from jax.sharding import PartitionSpec as P

TENSOR = ("zf", "zn", "y")
MESH_ID = pl.DeviceIdType.MESH
TILES = 128
GRAM_TILES = 48
CROSS_TILES = 32
PANEL = 32

momentum_decay = 0.95
step_rate = 0.02
norm_eps = 1e-06


def dot(left, right, dims):
    return lax.dot_general(
        left,
        right,
        (dims, ((), ())),
        precision=lax.Precision.HIGHEST,
        preferred_element_type=jnp.float32,
    )


def far_first(n):
    return sorted(range(1, n), key=lambda d: -min(d, n - d)) + [0]


def remote(src, dst, send, recv, device):
    copy = pltpu.make_async_remote_copy(
        src_ref=src,
        dst_ref=dst,
        send_sem=send,
        recv_sem=recv,
        device_id=device,
        device_id_type=MESH_ID,
    )
    copy.start()


def drain(ref, sem):
    pltpu.make_async_copy(ref, ref, sem).wait()


def greet(peers):
    barrier = pltpu.get_barrier_semaphore()
    for peer in peers:
        pl.semaphore_signal(barrier, inc=1, device_id=peer, device_id_type=MESH_ID)
    return lambda: pl.semaphore_wait(barrier, len(peers))


def others(axis, n, steps=None):
    me = lax.axis_index(axis)
    return [{axis: (me + d) % n} for d in (range(1, n) if steps is None else steps)]


def sum_over(axis, n, part, got, total, per, sems):
    me = lax.axis_index(axis)

    def scatter():
        for d in range(1, n):
            k = (me + d) % n
            remote(part.at[pl.ds(k * per, per)], got.at[d - 1], sems.at[0], sems.at[1], {axis: k})

    def gather():
        drain(got, sems.at[1])
        mine = part[pl.ds(me * per, per)]
        for d in range(1, n):
            mine = mine + got[d - 1]
        own = total.at[pl.ds(me * per, per)]
        own[...] = mine
        for d in range(1, n):
            remote(own, own, sems.at[2], sems.at[3], {axis: (me + d) % n})

    def finish():
        drain(got, sems.at[0])
        drain(got, sems.at[2])
        drain(got, sems.at[3])

    return scatter, gather, finish


def eliminate_panel(value, lo):
    sub = lax.broadcasted_iota(jnp.int32, (8, 128), 0)
    groups = PANEL // 8
    rows = [[value[8 * v : 8 * v + 8, 128 * c : 128 * (c + 1)] for c in range(3)] for v in range(groups)]
    cols = [
        {v: jnp.broadcast_to(rows[v][0][:, lo + j : lo + j + 1], (8, 128)) for v in range(j // 8, groups)}
        for j in range(PANEL)
    ]
    for j in range(PANEL):
        top_group, s = j // 8, j % 8
        scale = lax.rsqrt(cols[j][top_group][s : s + 1, :])
        factor = {v: cols[j][v] * scale for v in range(top_group, groups)}
        for k in range(j + 1, PANEL):
            mult = factor[k // 8][k % 8 : k % 8 + 1, :]
            for v in range(k // 8, groups):
                cols[k][v] = cols[k][v] - factor[v] * mult
        below = jnp.where(sub > s, factor[top_group], 0.0)
        for c in range(3):
            top = rows[top_group][c][s : s + 1, :] * scale
            rows[top_group][c] = jnp.where(sub == s, top, rows[top_group][c] - below * top)
            for v in range(top_group + 1, groups):
                rows[v][c] = rows[v][c] - factor[v] * top
    return jnp.concatenate([jnp.concatenate(row, axis=1) for row in rows], axis=0)


def eliminate(m):
    value = m[0:PANEL, :]
    for lo in range(0, 128, PANEL):
        hi, after = lo + PANEL, lo + 2 * PANEL
        done = eliminate_panel(value, lo)
        m[lo:hi, :] = done
        if hi < 128:
            value = m[hi:after, :] - dot(done[:, hi:after], done, ((0,), (0,)))
        if after < 128:
            m[after:128, :] = m[after:128, :] - dot(done[:, after:128], done, ((0,), (0,)))


def step_kernel(
    sizes,
    factor,
    weight_hbm,
    momentum_hbm,
    grad_hbm,
    q_hbm,
    new_weight_ref,
    new_momentum_ref,
    new_q_ref,
    weight_ref,
    momentum_ref,
    grad_ref,
    q_ref,
    part,
    full,
    got_y,
    got_n,
    sum_y,
    sum_n,
    ring_left,
    ring_right,
    out_left,
    out_right,
    gram_part,
    gram_got,
    gram_total,
    cross_part,
    cross_got,
    cross_total,
    m,
    square,
    square_y,
    square_z,
    rs_send,
    rs_y,
    rs_n,
    rs_left,
    rs_right,
    ag_send,
    ag_y,
    ag_n,
    ag_f,
    gram_sem,
    cross_sem,
    square_sem,
    load_sem,
):
    n_fsdp, n_f, n_n, n_y = sizes
    unit = TILES // (n_f * n_n * n_y)
    f_me, n_me, y_me = lax.axis_index("zf"), lax.axis_index("zn"), lax.axis_index("y")
    order = far_first(n_f)
    far = n_f // 2
    half = TILES // 2

    def chunk(f, y):
        return pl.ds((f * n_y + y) * (n_n * unit), n_n * unit)

    def tile(f, n, y):
        return pl.ds(((f * n_y + y) * n_n + n) * unit, unit)

    entered = greet(
        others("y", n_y)
        + others("zn", n_n)
        + others("zf", n_f, sorted({1, n_f - 1}))
        + others("fsdp", n_fsdp)
    )
    loads = [
        pltpu.make_async_copy(src, dst, load_sem.at[i])
        for i, (src, dst) in enumerate(
            ((momentum_hbm, momentum_ref), (grad_hbm, grad_ref), (q_hbm, q_ref), (weight_hbm, weight_ref))
        )
    ]
    for load in loads:
        load.start()
    for load in loads[:3]:
        load.wait()
    buffer = momentum_ref[...] + grad_ref[...].astype(jnp.float32)
    local = dot(buffer, q_ref[...], ((0,), (0,)))
    part[0:half] = local[:, 0:128].reshape(half, 8, 128)
    part[half:TILES] = local[:, 128:256].reshape(half, 8, 128)
    entered()

    for i, d in enumerate(order):
        f = (f_me + d) % n_f
        for e in range(1, n_y):
            y = (y_me + e) % n_y
            remote(part.at[chunk(f, y)], got_y.at[i, e - 1], rs_send.at[0], rs_y.at[i], {"y": y})

    def after_y(i):
        drain(got_y.at[i], rs_y.at[i])
        total = part[chunk((f_me + order[i]) % n_f, y_me)]
        for e in range(1, n_y):
            total = total + got_y[i, e - 1]
        sum_y[i] = total
        for e in range(1, n_n):
            n = (n_me + e) % n_n
            remote(
                sum_y.at[i, pl.ds(n * unit, unit)], got_n.at[i, e - 1], rs_send.at[1], rs_n.at[i], {"zn": n}
            )

    left = ((f_me + n_f - 1) % n_f, ring_left, out_left, rs_left, rs_send.at[2], far, lambda s: far + s)
    right = (
        (f_me + 1) % n_f,
        ring_right,
        out_right,
        rs_right,
        rs_send.at[3],
        n_f - 1 - far,
        lambda s: n_f - 1 - far - s,
    )

    def ring_step(way, s):
        peer, ring, out, recv, send, length, piece = way
        if s < length:
            value = sum_n[order.index(piece(s))]
            if s:
                drain(ring.at[s - 1], recv.at[s - 1])
                value = value + ring[s - 1]
            out[s] = value
            remote(out.at[s], ring.at[s], send, recv.at[s], {"zf": peer})

    def after_n(i):
        drain(got_n.at[i], rs_n.at[i])
        total = sum_y[i, pl.ds(n_me * unit, unit)]
        for e in range(1, n_n):
            total = total + got_n[i, e - 1]
        sum_n[i] = total
        for way in (left, right):
            if way[5] and order[i] == way[6](0):
                ring_step(way, 0)

    lag = n_f // 2
    for i in range(n_f + lag):
        if i < n_f:
            after_y(i)
        if i >= lag:
            after_n(i - lag)
    for s in range(1, far):
        ring_step(left, s)
        ring_step(right, s)
    total = sum_n[n_f - 1]
    for peer, ring, out, recv, send, length, piece in (left, right):
        if length:
            drain(ring.at[length - 1], recv.at[length - 1])
            total = total + ring[length - 1]

    own = full.at[tile(f_me, n_me, y_me)]
    own[...] = total
    for n in range(n_n):
        peer = {"zf": (f_me + far) % n_f, "zn": (n_me + n) % n_n}
        remote(own, own, ag_send.at[0], ag_f.at[far], peer)
    for d in order[1:-1]:
        remote(own, own, ag_send.at[0], ag_f.at[d], {"zf": (f_me + d) % n_f})

    def spread_n(d):
        mine = full.at[tile((f_me - d + n_f) % n_f, n_me, y_me)]
        if d:
            drain(mine, ag_f.at[d])
        for e in range(1, n_n):
            remote(mine, mine, ag_send.at[1], ag_n.at[d], {"zn": (n_me + e) % n_n})

    def spread_y(d):
        mine = full.at[chunk((f_me - d + n_f) % n_f, y_me)]
        if d == far:
            drain(mine, ag_f.at[d])
        else:
            drain(full.at[0 : (n_n - 1) * unit], ag_n.at[d])
        for e in range(1, n_y):
            remote(mine, mine, ag_send.at[2], ag_y, {"y": (y_me + e) % n_y})

    near = order[:0:-1]
    lag = min(3, n_f - 1)
    for i in range(n_f - 1 + lag):
        if i < n_f - 1:
            spread_n(near[i])
        if i == n_f:
            spread_y(far)
        if i >= lag:
            spread_y(near[i - lag])
    if n_f - 1 + lag <= n_f:
        spread_y(far)
    drain(full.at[0 : TILES // n_y * (n_y - 1)], ag_y)

    whole = jnp.concatenate(
        [full[0:half].reshape(half * 8, 128), full[half:TILES].reshape(half * 8, 128)], axis=1
    )
    gram = dot(whole, whole, ((0,), (0,)))
    for i, (r, c) in enumerate(((0, 0), (0, 1), (1, 1))):
        block = gram[r * 128 : (r + 1) * 128, c * 128 : (c + 1) * 128]
        gram_part[i * 16 : (i + 1) * 16] = block.reshape(16, 8, 128)
    gram_scatter, gram_gather, gram_finish = sum_over(
        "fsdp", n_fsdp, gram_part, gram_got, gram_total, GRAM_TILES // n_fsdp, gram_sem
    )
    cross_scatter, cross_gather, cross_finish = sum_over(
        "fsdp", n_fsdp, cross_part, cross_got, cross_total, CROSS_TILES // n_fsdp, cross_sem
    )
    gram_scatter()
    cross = dot(buffer, whole, ((1,), (0,)))
    cross_part[0:14] = cross[:, 0:128].reshape(14, 8, 128)
    cross_part[14:28] = cross[:, 128:256].reshape(14, 8, 128)
    cross_part[28:32] = jnp.zeros((4, 8, 128), jnp.float32)
    gram_gather()
    cross_scatter()
    gram_finish()

    eye = (
        lax.broadcasted_iota(jnp.int32, (128, 128), 0) == lax.broadcasted_iota(jnp.int32, (128, 128), 1)
    ).astype(jnp.float32)
    m[:, 0:128] = gram_total[0:16].reshape(128, 128)
    m[:, 128:256] = gram_total[16:32].reshape(128, 128)
    m[:, 256:384] = eye
    eliminate(m)
    cross_gather()
    across, first = m[:, 128:256], m[:, 256:384]
    m[:, 0:128] = gram_total[32:48].reshape(128, 128) - dot(across, across, ((0,), (0,)))
    m[:, 128:256] = -dot(across, first, ((0,), (0,)))
    m[:, 256:384] = eye
    eliminate(m)
    inverse = jnp.concatenate(
        [jnp.concatenate([first, jnp.zeros_like(first)], axis=1), m[:, 128:384]], axis=0
    )
    cross_finish()
    cross = jnp.concatenate(
        [cross_total[0:14].reshape(112, 128), cross_total[14:28].reshape(112, 128)], axis=1
    )
    right_factor = dot(cross, inverse, ((1,), (1,)))

    value = jnp.sum(right_factor * right_factor, axis=0, keepdims=True)
    square[0] = value
    for d in range(1, n_y):
        remote(square.at[0], square_y.at[d - 1], square_sem.at[0], square_sem.at[1], {"y": (y_me + d) % n_y})
    ortho = dot(whole, inverse, ((1,), (1,)))
    drain(square_y, square_sem.at[1])
    for d in range(1, n_y):
        value = value + square_y[d - 1]
    square[1] = value
    n_z = n_f * n_n
    z_me = f_me * n_n + n_me
    for d in far_first(n_z)[:-1]:
        z = (z_me + d) % n_z
        peer = {"zf": z // n_n, "zn": z % n_n}
        remote(square.at[1], square_z.at[d - 1], square_sem.at[2], square_sem.at[3], peer)
    new_momentum_ref[...] = buffer - (1.0 - momentum_decay) * dot(right_factor, ortho, ((1,), (1,)))

    drain(part.at[0 : TILES // n_y * (n_y - 1)], rs_send.at[0])
    drain(got_n, rs_send.at[1])
    for peer, ring, out, recv, send, length, piece in (left, right):
        if length:
            drain(out.at[0:length], send)
    drain(full.at[0 : (n_f - 2 + n_n) * unit], ag_send.at[0])
    drain(full.at[0 : (n_f - 1) * (n_n - 1) * unit], ag_send.at[1])
    drain(full.at[0 : TILES // n_y * (n_y - 1)], ag_send.at[2])
    drain(square_y, square_sem.at[0])
    drain(square_z, square_sem.at[3])
    drain(square_z, square_sem.at[2])
    loads[3].wait()
    for d in range(1, n_z):
        value = value + square_z[d - 1]
    q_new = right_factor / (jnp.sqrt(value) + norm_eps)
    new_q_ref[...] = q_new
    update = dot(q_new, ortho, ((1,), (1,)))
    new_weight_ref[...] = (weight_ref[...].astype(jnp.float32) - factor * update).astype(jnp.bfloat16)


def store_kernel(*refs):
    values, outs, sem = refs[:3], refs[3:6], refs[6]
    copies = [pltpu.make_async_copy(v, o, sem.at[i]) for i, (v, o) in enumerate(zip(values, outs))]
    for copy in copies:
        copy.start()
    for copy in copies:
        copy.wait()


def per_device(sizes, factor, weight, momentum, grad, q_prev):
    n_fsdp, n_f, n_n, n_y = sizes
    unit = TILES // (n_f * n_n * n_y)
    far = n_f // 2
    vmem = pl.BlockSpec(memory_space=pltpu.VMEM)
    hbm = pl.BlockSpec(memory_space=pltpu.HBM)
    dma = pltpu.SemaphoreType.DMA

    def tiles(*shape):
        return pltpu.VMEM((*shape, 8, 128), jnp.float32)

    def row(*shape):
        return pltpu.VMEM((*shape, 1, 256), jnp.float32)

    gram_per, cross_per = GRAM_TILES // n_fsdp, CROSS_TILES // n_fsdp
    outs = (
        jax.ShapeDtypeStruct(weight.shape, jnp.bfloat16),
        jax.ShapeDtypeStruct(momentum.shape, jnp.float32),
        jax.ShapeDtypeStruct(q_prev.shape, jnp.float32),
    )
    results = pl.pallas_call(
        functools.partial(step_kernel, sizes, factor),
        out_shape=outs,
        in_specs=[hbm] * 4,
        out_specs=(vmem,) * 3,
        scratch_shapes=[
            pltpu.VMEM(weight.shape, weight.dtype),
            pltpu.VMEM(momentum.shape, momentum.dtype),
            pltpu.VMEM(grad.shape, grad.dtype),
            pltpu.VMEM(q_prev.shape, q_prev.dtype),
            tiles(TILES),
            tiles(TILES),
            tiles(n_f, n_y - 1, n_n * unit),
            tiles(n_f, n_n - 1, unit),
            tiles(n_f, n_n * unit),
            tiles(n_f, unit),
            tiles(far, unit),
            tiles(far, unit),
            tiles(far, unit),
            tiles(far, unit),
            tiles(GRAM_TILES),
            tiles(n_fsdp - 1, gram_per),
            tiles(GRAM_TILES),
            tiles(CROSS_TILES),
            tiles(n_fsdp - 1, cross_per),
            tiles(CROSS_TILES),
            pltpu.VMEM((128, 384), jnp.float32),
            row(2),
            row(n_y - 1),
            row(n_f * n_n - 1),
            dma((4,)),
            dma((n_f,)),
            dma((n_f,)),
            dma((far,)),
            dma((far,)),
            dma((3,)),
            dma,
            dma((n_f,)),
            dma((n_f,)),
            dma((4,)),
            dma((4,)),
            dma((4,)),
            dma((4,)),
        ],
        compiler_params=pltpu.CompilerParams(
            collective_id=0, has_side_effects=True, vmem_limit_bytes=24 << 20
        ),
        name="step",
    )(*(pltpu.with_memory_space_constraint(x, pltpu.HBM) for x in (weight, momentum, grad, q_prev)))
    return pl.pallas_call(
        store_kernel,
        out_shape=outs,
        in_specs=[vmem] * 3,
        out_specs=(hbm,) * 3,
        scratch_shapes=[dma((3,))],
        compiler_params=pltpu.CompilerParams(vmem_limit_bytes=4 << 20),
        name="store",
    )(*results)


def split_tensor(n):
    return (8, 4, 4) if n == 128 else (n // 4, 2, 2)


def solution(mesh):
    n_fsdp, n_tensor = mesh.shape["fsdp"], mesh.shape["tensor"]
    sizes = (n_fsdp, *split_tensor(n_tensor))
    torus = Mesh(mesh.devices.reshape(sizes), ("fsdp", *TENSOR))
    factor = step_rate * math.sqrt(14336 / 4096)
    return jax.shard_map(
        functools.partial(per_device, sizes, factor),
        mesh=torus,
        in_specs=(P(TENSOR, "fsdp"), P(TENSOR, "fsdp"), P(TENSOR, "fsdp"), P(TENSOR, None)),
        out_specs=(P(TENSOR, "fsdp"), P(TENSOR, "fsdp"), P(TENSOR, None)),
        check_vma=False,
    )
```

```python
import functools
import math

import jax
import jax.numpy as jnp
from jax import lax
from jax.experimental import pallas as pl
from jax.experimental.pallas import tpu as pltpu
from jax.sharding import Mesh
from jax.sharding import PartitionSpec as P

TENSOR = ("zf", "zn", "y")
MESH_ID = pl.DeviceIdType.MESH
TILES = 128
FIRST_TILES = 32
SECOND_TILES = 16
CROSS_TILES = 32
PANEL = 32

momentum_decay = 0.95
step_rate = 0.02
norm_eps = 1e-06


def dot(left, right, dims):
    return lax.dot_general(
        left,
        right,
        (dims, ((), ())),
        precision=lax.Precision.HIGHEST,
        preferred_element_type=jnp.float32,
    )


def far_first(n):
    return sorted(range(1, n), key=lambda d: -min(d, n - d)) + [0]


def remote(src, dst, send, recv, device):
    copy = pltpu.make_async_remote_copy(
        src_ref=src,
        dst_ref=dst,
        send_sem=send,
        recv_sem=recv,
        device_id=device,
        device_id_type=MESH_ID,
    )
    copy.start()


def drain(ref, sem):
    pltpu.make_async_copy(ref, ref, sem).wait()


def greet(peers):
    barrier = pltpu.get_barrier_semaphore()
    for peer in peers:
        pl.semaphore_signal(barrier, inc=1, device_id=peer, device_id_type=MESH_ID)
    return lambda: pl.semaphore_wait(barrier, len(peers))


def others(axis, n, steps=None):
    me = lax.axis_index(axis)
    return [{axis: (me + d) % n} for d in (range(1, n) if steps is None else steps)]


def sum_over(axis, n, part, got, total, per, sems):
    me = lax.axis_index(axis)

    def scatter():
        for d in range(1, n):
            k = (me + d) % n
            remote(part.at[pl.ds(k * per, per)], got.at[d - 1], sems.at[0], sems.at[1], {axis: k})

    def gather():
        drain(got, sems.at[1])
        mine = part[pl.ds(me * per, per)]
        for d in range(1, n):
            mine = mine + got[d - 1]
        own = total.at[pl.ds(me * per, per)]
        own[...] = mine
        for d in range(1, n):
            remote(own, own, sems.at[2], sems.at[3], {axis: (me + d) % n})

    def finish():
        drain(got, sems.at[0])
        drain(got, sems.at[2])
        drain(got, sems.at[3])

    return scatter, gather, finish


def eliminate_panel(value, lo):
    sub = lax.broadcasted_iota(jnp.int32, (8, 128), 0)
    groups = PANEL // 8
    rows = [[value[8 * v : 8 * v + 8, 128 * c : 128 * (c + 1)] for c in range(3)] for v in range(groups)]
    cols = [
        {v: jnp.broadcast_to(rows[v][0][:, lo + j : lo + j + 1], (8, 128)) for v in range(j // 8, groups)}
        for j in range(PANEL)
    ]
    for j in range(PANEL):
        top_group, s = j // 8, j % 8
        scale = lax.rsqrt(cols[j][top_group][s : s + 1, :])
        factor = {v: cols[j][v] * scale for v in range(top_group, groups)}
        for k in range(j + 1, PANEL):
            mult = factor[k // 8][k % 8 : k % 8 + 1, :]
            for v in range(k // 8, groups):
                cols[k][v] = cols[k][v] - factor[v] * mult
        below = jnp.where(sub > s, factor[top_group], 0.0)
        for c in range(3):
            top = rows[top_group][c][s : s + 1, :] * scale
            rows[top_group][c] = jnp.where(sub == s, top, rows[top_group][c] - below * top)
            for v in range(top_group + 1, groups):
                rows[v][c] = rows[v][c] - factor[v] * top
    return jnp.concatenate([jnp.concatenate(row, axis=1) for row in rows], axis=0)


def eliminate(m):
    value = m[0:PANEL, :]
    for lo in range(0, 128, PANEL):
        hi, after = lo + PANEL, lo + 2 * PANEL
        done = eliminate_panel(value, lo)
        m[lo:hi, :] = done
        if hi < 128:
            value = m[hi:after, :] - dot(done[:, hi:after], done, ((0,), (0,)))
        if after < 128:
            m[after:128, :] = m[after:128, :] - dot(done[:, after:128], done, ((0,), (0,)))


def step_kernel(
    sizes,
    factor,
    weight_hbm,
    momentum_hbm,
    grad_hbm,
    q_hbm,
    new_weight_ref,
    new_momentum_ref,
    new_q_ref,
    weight_ref,
    momentum_ref,
    grad_ref,
    q_ref,
    part,
    full,
    got_y,
    got_n,
    sum_y,
    sum_n,
    got_f,
    first_part,
    first_got,
    first_total,
    second_part,
    second_got,
    second_total,
    cross_part,
    cross_got,
    cross_total,
    m,
    square,
    square_y,
    square_z,
    rs_send,
    rs_y,
    rs_n,
    rs_f,
    ag_send,
    ag_y,
    ag_n,
    ag_f,
    first_sem,
    second_sem,
    cross_sem,
    square_sem,
    load_sem,
    relay,
):
    n_fsdp, n_f, n_n, n_y = sizes
    unit = TILES // (n_f * n_n * n_y)
    f_me, n_me, y_me = lax.axis_index("zf"), lax.axis_index("zn"), lax.axis_index("y")
    order = far_first(n_f)
    far = n_f // 2
    half = TILES // 2

    def chunk(f, y):
        return pl.ds((f * n_y + y) * (n_n * unit), n_n * unit)

    def tile(f, n, y):
        return pl.ds(((f * n_y + y) * n_n + n) * unit, unit)

    entered = greet(
        others("y", n_y)
        + others("zn", n_n)
        + others("zf", n_f, sorted({1, n_f - 1}))
        + others("fsdp", n_fsdp)
    )
    loads = [
        pltpu.make_async_copy(src, dst, load_sem.at[i])
        for i, (src, dst) in enumerate(
            ((momentum_hbm, momentum_ref), (grad_hbm, grad_ref), (q_hbm, q_ref), (weight_hbm, weight_ref))
        )
    ]
    for load in loads:
        load.start()
    for load in loads[:3]:
        load.wait()
    buffer = momentum_ref[...] + grad_ref[...].astype(jnp.float32)
    local = dot(buffer, q_ref[...], ((0,), (0,)))
    part[0:half] = local[:, 0:128].reshape(half, 8, 128)
    part[half:TILES] = local[:, 128:256].reshape(half, 8, 128)
    entered()

    def pass_on(k):
        for peer in relayed[k]:
            pl.semaphore_signal(relay.at[k], inc=1, device_id=peer, device_id_type=MESH_ID)

    def passed_on(k):
        pl.semaphore_wait(relay.at[k], len(relayed[k]))

    steps = [1 << k for k in range(8) if 1 << k < far]
    relayed = [others("zf", n_f, sorted({step, n_f - step})) for step in steps]
    if steps:
        pass_on(0)

    for i, d in enumerate(order):
        f = (f_me + d) % n_f
        for e in range(1, n_y):
            y = (y_me + e) % n_y
            remote(part.at[chunk(f, y)], got_y.at[i, e - 1], rs_send.at[0], rs_y.at[i], {"y": y})
    for k in range(1, len(steps)):
        passed_on(k - 1)
        pass_on(k)

    def after_y(i):
        drain(got_y.at[i], rs_y.at[i])
        total = part[chunk((f_me + order[i]) % n_f, y_me)]
        for e in range(1, n_y):
            total = total + got_y[i, e - 1]
        sum_y[i] = total
        for e in range(1, n_n):
            n = (n_me + e) % n_n
            share = sum_y.at[i, pl.ds(n * unit, unit)]
            remote(share, got_n.at[i, e - 1], rs_send.at[1], rs_n.at[i], {"zn": n})

    def after_n(i):
        drain(got_n.at[i], rs_n.at[i])
        total = sum_y[i, pl.ds(n_me * unit, unit)]
        for e in range(1, n_n):
            total = total + got_n[i, e - 1]
        sum_n[i] = total
        d = order[i]
        if d:
            remote(sum_n.at[i], got_f.at[i], rs_send.at[2], rs_f, {"zf": (f_me + d) % n_f})

    waiting = list(range(n_f))
    for i in range(min(n_f, 6)):
        after_y(waiting.pop(0))
    if steps:
        passed_on(len(steps) - 1)
    for i in range(n_f):
        if i >= 3 and waiting:
            after_y(waiting.pop(0))
        after_n(i)
    total = sum_n[n_f - 1]
    drain(got_f, rs_f)
    for i in range(n_f - 1):
        total = total + got_f[i]

    own = full.at[tile(f_me, n_me, y_me)]
    own[...] = total
    for n in range(n_n):
        peer = {"zf": (f_me + far) % n_f, "zn": (n_me + n) % n_n}
        remote(own, own, ag_send.at[0], ag_f.at[far], peer)
    for d in order[1:-1]:
        remote(own, own, ag_send.at[0], ag_f.at[d], {"zf": (f_me + d) % n_f})

    def spread_n(d):
        mine = full.at[tile((f_me - d + n_f) % n_f, n_me, y_me)]
        if d:
            drain(mine, ag_f.at[d])
        for e in range(1, n_n):
            remote(mine, mine, ag_send.at[1], ag_n.at[d], {"zn": (n_me + e) % n_n})

    def spread_y(d):
        mine = full.at[chunk((f_me - d + n_f) % n_f, y_me)]
        if d == far:
            drain(mine, ag_f.at[d])
        else:
            drain(full.at[0 : (n_n - 1) * unit], ag_n.at[d])
        for e in range(1, n_y):
            remote(mine, mine, ag_send.at[2], ag_y, {"y": (y_me + e) % n_y})

    near = order[:0:-1]
    lag = min(3, n_f - 1)
    for i in range(n_f - 1 + lag):
        if i < n_f - 1:
            spread_n(near[i])
        if i == n_f:
            spread_y(far)
        if i >= lag:
            spread_y(near[i - lag])
    if n_f - 1 + lag <= n_f:
        spread_y(far)
    drain(full.at[0 : TILES // n_y * (n_y - 1)], ag_y)

    whole = jnp.concatenate(
        [full[0:half].reshape(half * 8, 128), full[half:TILES].reshape(half * 8, 128)], axis=1
    )
    gram = dot(whole, whole, ((0,), (0,)))
    first_part[0:16] = gram[0:128, 0:128].reshape(16, 8, 128)
    first_part[16:32] = gram[0:128, 128:256].reshape(16, 8, 128)
    second_part[...] = gram[128:256, 128:256].reshape(16, 8, 128)
    first_scatter, first_gather, first_finish = sum_over(
        "fsdp", n_fsdp, first_part, first_got, first_total, FIRST_TILES // n_fsdp, first_sem
    )
    second_scatter, second_gather, second_finish = sum_over(
        "fsdp", n_fsdp, second_part, second_got, second_total, SECOND_TILES // n_fsdp, second_sem
    )
    cross_scatter, cross_gather, cross_finish = sum_over(
        "fsdp", n_fsdp, cross_part, cross_got, cross_total, CROSS_TILES // n_fsdp, cross_sem
    )
    first_scatter()
    cross = dot(buffer, whole, ((1,), (0,)))
    cross_part[0:14] = cross[:, 0:128].reshape(14, 8, 128)
    cross_part[14:28] = cross[:, 128:256].reshape(14, 8, 128)
    cross_part[28:32] = jnp.zeros((4, 8, 128), jnp.float32)
    first_gather()
    second_scatter()
    first_finish()
    second_gather()
    cross_scatter()

    eye = (
        lax.broadcasted_iota(jnp.int32, (128, 128), 0) == lax.broadcasted_iota(jnp.int32, (128, 128), 1)
    ).astype(jnp.float32)
    m[:, 0:128] = first_total[0:16].reshape(128, 128)
    m[:, 128:256] = first_total[16:32].reshape(128, 128)
    m[:, 256:384] = eye
    eliminate(m)
    second_finish()
    cross_gather()
    across, first = m[:, 128:256], m[:, 256:384]
    m[:, 0:128] = second_total[...].reshape(128, 128) - dot(across, across, ((0,), (0,)))
    m[:, 128:256] = -dot(across, first, ((0,), (0,)))
    m[:, 256:384] = eye
    eliminate(m)
    inverse = jnp.concatenate(
        [jnp.concatenate([first, jnp.zeros_like(first)], axis=1), m[:, 128:384]], axis=0
    )
    cross_finish()
    cross = jnp.concatenate(
        [cross_total[0:14].reshape(112, 128), cross_total[14:28].reshape(112, 128)], axis=1
    )
    right_factor = dot(cross, inverse, ((1,), (1,)))

    value = jnp.sum(right_factor * right_factor, axis=0, keepdims=True)
    square[0] = value
    for d in range(1, n_y):
        remote(square.at[0], square_y.at[d - 1], square_sem.at[0], square_sem.at[1], {"y": (y_me + d) % n_y})
    ortho = dot(whole, inverse, ((1,), (1,)))
    drain(square_y, square_sem.at[1])
    for d in range(1, n_y):
        value = value + square_y[d - 1]
    square[1] = value
    n_z = n_f * n_n
    z_me = f_me * n_n + n_me
    for d in far_first(n_z)[:-1]:
        z = (z_me + d) % n_z
        peer = {"zf": z // n_n, "zn": z % n_n}
        remote(square.at[1], square_z.at[d - 1], square_sem.at[2], square_sem.at[3], peer)
    new_momentum_ref[...] = buffer - (1.0 - momentum_decay) * dot(right_factor, ortho, ((1,), (1,)))

    drain(part.at[0 : TILES // n_y * (n_y - 1)], rs_send.at[0])
    drain(got_n, rs_send.at[1])
    drain(got_f, rs_send.at[2])
    drain(full.at[0 : (n_f - 2 + n_n) * unit], ag_send.at[0])
    drain(full.at[0 : (n_f - 1) * (n_n - 1) * unit], ag_send.at[1])
    drain(full.at[0 : TILES // n_y * (n_y - 1)], ag_send.at[2])
    drain(square_y, square_sem.at[0])
    drain(square_z, square_sem.at[3])
    drain(square_z, square_sem.at[2])
    loads[3].wait()
    for d in range(1, n_z):
        value = value + square_z[d - 1]
    q_new = right_factor / (jnp.sqrt(value) + norm_eps)
    new_q_ref[...] = q_new
    update = dot(q_new, ortho, ((1,), (1,)))
    new_weight_ref[...] = (weight_ref[...].astype(jnp.float32) - factor * update).astype(jnp.bfloat16)


def store_kernel(*refs):
    values, outs, sem = refs[:3], refs[3:6], refs[6]
    copies = [pltpu.make_async_copy(v, o, sem.at[i]) for i, (v, o) in enumerate(zip(values, outs))]
    for copy in copies:
        copy.start()
    for copy in copies:
        copy.wait()


def per_device(sizes, factor, weight, momentum, grad, q_prev):
    n_fsdp, n_f, n_n, n_y = sizes
    unit = TILES // (n_f * n_n * n_y)
    vmem = pl.BlockSpec(memory_space=pltpu.VMEM)
    hbm = pl.BlockSpec(memory_space=pltpu.HBM)
    dma = pltpu.SemaphoreType.DMA

    def tiles(*shape):
        return pltpu.VMEM((*shape, 8, 128), jnp.float32)

    def row(*shape):
        return pltpu.VMEM((*shape, 1, 256), jnp.float32)

    outs = (
        jax.ShapeDtypeStruct(weight.shape, jnp.bfloat16),
        jax.ShapeDtypeStruct(momentum.shape, jnp.float32),
        jax.ShapeDtypeStruct(q_prev.shape, jnp.float32),
    )
    results = pl.pallas_call(
        functools.partial(step_kernel, sizes, factor),
        out_shape=outs,
        in_specs=[hbm] * 4,
        out_specs=(vmem,) * 3,
        scratch_shapes=[
            pltpu.VMEM(weight.shape, weight.dtype),
            pltpu.VMEM(momentum.shape, momentum.dtype),
            pltpu.VMEM(grad.shape, grad.dtype),
            pltpu.VMEM(q_prev.shape, q_prev.dtype),
            tiles(TILES),
            tiles(TILES),
            tiles(n_f, n_y - 1, n_n * unit),
            tiles(n_f, n_n - 1, unit),
            tiles(n_f, n_n * unit),
            tiles(n_f, unit),
            tiles(n_f - 1, unit),
            tiles(FIRST_TILES),
            tiles(n_fsdp - 1, FIRST_TILES // n_fsdp),
            tiles(FIRST_TILES),
            tiles(SECOND_TILES),
            tiles(n_fsdp - 1, SECOND_TILES // n_fsdp),
            tiles(SECOND_TILES),
            tiles(CROSS_TILES),
            tiles(n_fsdp - 1, CROSS_TILES // n_fsdp),
            tiles(CROSS_TILES),
            pltpu.VMEM((128, 384), jnp.float32),
            row(2),
            row(n_y - 1),
            row(n_f * n_n - 1),
            dma((3,)),
            dma((n_f,)),
            dma((n_f,)),
            dma,
            dma((3,)),
            dma,
            dma((n_f,)),
            dma((n_f,)),
            dma((4,)),
            dma((4,)),
            dma((4,)),
            dma((4,)),
            dma((4,)),
            pltpu.SemaphoreType.REGULAR((2,)),
        ],
        compiler_params=pltpu.CompilerParams(
            collective_id=0, has_side_effects=True, vmem_limit_bytes=24 << 20
        ),
        name="step",
    )(*(pltpu.with_memory_space_constraint(x, pltpu.HBM) for x in (weight, momentum, grad, q_prev)))
    return pl.pallas_call(
        store_kernel,
        out_shape=outs,
        in_specs=[vmem] * 3,
        out_specs=(hbm,) * 3,
        scratch_shapes=[dma((3,))],
        compiler_params=pltpu.CompilerParams(vmem_limit_bytes=4 << 20),
        name="store",
    )(*results)


def split_tensor(n):
    return (8, 4, 4) if n == 128 else (n // 4, 2, 2)


def solution(mesh):
    n_fsdp, n_tensor = mesh.shape["fsdp"], mesh.shape["tensor"]
    sizes = (n_fsdp, *split_tensor(n_tensor))
    torus = Mesh(mesh.devices.reshape(sizes), ("fsdp", *TENSOR))
    factor = step_rate * math.sqrt(14336 / 4096)
    return jax.shard_map(
        functools.partial(per_device, sizes, factor),
        mesh=torus,
        in_specs=(P(TENSOR, "fsdp"), P(TENSOR, "fsdp"), P(TENSOR, "fsdp"), P(TENSOR, None)),
        out_specs=(P(TENSOR, "fsdp"), P(TENSOR, "fsdp"), P(TENSOR, None)),
        check_vma=False,
    )
```

```python
import functools
import math

import jax
import jax.numpy as jnp
from jax import lax
from jax.experimental import pallas as pl
from jax.experimental.pallas import tpu as pltpu
from jax.sharding import Mesh
from jax.sharding import PartitionSpec as P

TENSOR = ("zf", "zn", "y")
MESH_ID = pl.DeviceIdType.MESH
TILES = 128
FIRST_TILES = 32
SECOND_TILES = 16
CROSS_TILES = 32
PANEL = 32

momentum_decay = 0.95
step_rate = 0.02
norm_eps = 1e-06


def dot(left, right, dims):
    return lax.dot_general(
        left,
        right,
        (dims, ((), ())),
        precision=lax.Precision.HIGHEST,
        preferred_element_type=jnp.float32,
    )


def far_first(n):
    return sorted(range(1, n), key=lambda d: -min(d, n - d)) + [0]


def remote(src, dst, send, recv, device):
    copy = pltpu.make_async_remote_copy(
        src_ref=src,
        dst_ref=dst,
        send_sem=send,
        recv_sem=recv,
        device_id=device,
        device_id_type=MESH_ID,
    )
    copy.start()


def drain(ref, sem):
    pltpu.make_async_copy(ref, ref, sem).wait()


def greet(peers):
    barrier = pltpu.get_barrier_semaphore()
    for peer in peers:
        pl.semaphore_signal(barrier, inc=1, device_id=peer, device_id_type=MESH_ID)
    return lambda: pl.semaphore_wait(barrier, len(peers))


def others(axis, n, steps=None):
    me = lax.axis_index(axis)
    return [{axis: (me + d) % n} for d in (range(1, n) if steps is None else steps)]


def sum_over(axis, n, part, got, total, per, sems):
    me = lax.axis_index(axis)

    def scatter():
        for d in range(1, n):
            k = (me + d) % n
            remote(part.at[pl.ds(k * per, per)], got.at[d - 1], sems.at[0], sems.at[1], {axis: k})

    def gather():
        drain(got, sems.at[1])
        mine = part[pl.ds(me * per, per)]
        for d in range(1, n):
            mine = mine + got[d - 1]
        own = total.at[pl.ds(me * per, per)]
        own[...] = mine
        for d in range(1, n):
            remote(own, own, sems.at[2], sems.at[3], {axis: (me + d) % n})

    def finish():
        drain(got, sems.at[0])
        drain(got, sems.at[2])
        drain(got, sems.at[3])

    return scatter, gather, finish


def eliminate_panel(value, lo):
    sub = lax.broadcasted_iota(jnp.int32, (8, 128), 0)
    groups = PANEL // 8
    rows = [[value[8 * v : 8 * v + 8, 128 * c : 128 * (c + 1)] for c in range(3)] for v in range(groups)]
    cols = [
        {v: jnp.broadcast_to(rows[v][0][:, lo + j : lo + j + 1], (8, 128)) for v in range(j // 8, groups)}
        for j in range(PANEL)
    ]
    for j in range(PANEL):
        top_group, s = j // 8, j % 8
        scale = lax.rsqrt(cols[j][top_group][s : s + 1, :])
        factor = {v: cols[j][v] * scale for v in range(top_group, groups)}
        for k in range(j + 1, PANEL):
            mult = factor[k // 8][k % 8 : k % 8 + 1, :]
            for v in range(k // 8, groups):
                cols[k][v] = cols[k][v] - factor[v] * mult
        below = jnp.where(sub > s, factor[top_group], 0.0)
        for c in range(3):
            top = rows[top_group][c][s : s + 1, :] * scale
            rows[top_group][c] = jnp.where(sub == s, top, rows[top_group][c] - below * top)
            for v in range(top_group + 1, groups):
                rows[v][c] = rows[v][c] - factor[v] * top
    return jnp.concatenate([jnp.concatenate(row, axis=1) for row in rows], axis=0)


def eliminate(m):
    value = m[0:PANEL, :]
    for lo in range(0, 128, PANEL):
        hi, after = lo + PANEL, lo + 2 * PANEL
        done = eliminate_panel(value, lo)
        m[lo:hi, :] = done
        if hi < 128:
            value = m[hi:after, :] - dot(done[:, hi:after], done, ((0,), (0,)))
        if after < 128:
            m[after:128, :] = m[after:128, :] - dot(done[:, after:128], done, ((0,), (0,)))


def step_kernel(
    sizes,
    factor,
    weight_hbm,
    momentum_hbm,
    grad_hbm,
    q_hbm,
    new_weight_ref,
    new_momentum_ref,
    new_q_ref,
    weight_ref,
    momentum_ref,
    grad_ref,
    q_ref,
    part,
    full,
    got_y,
    got_n,
    sum_y,
    sum_n,
    got_f,
    first_part,
    first_got,
    first_total,
    second_part,
    second_got,
    second_total,
    cross_part,
    cross_got,
    cross_total,
    m,
    square,
    square_y,
    square_z,
    rs_send,
    rs_y,
    rs_n,
    rs_f,
    ag_send,
    ag_y,
    ag_n,
    ag_f,
    first_sem,
    second_sem,
    cross_sem,
    square_sem,
    load_sem,
    relay,
):
    n_fsdp, n_f, n_n, n_y = sizes
    unit = TILES // (n_f * n_n * n_y)
    f_me, n_me, y_me = lax.axis_index("zf"), lax.axis_index("zn"), lax.axis_index("y")
    order = far_first(n_f)
    far = n_f // 2
    half = TILES // 2

    def chunk(f, y):
        return pl.ds((f * n_y + y) * (n_n * unit), n_n * unit)

    def tile(f, n, y):
        return pl.ds(((f * n_y + y) * n_n + n) * unit, unit)

    entered = greet(
        others("y", n_y)
        + others("zn", n_n)
        + others("zf", n_f, sorted({1, n_f - 1}))
        + others("fsdp", n_fsdp)
    )
    loads = [
        pltpu.make_async_copy(src, dst, load_sem.at[i])
        for i, (src, dst) in enumerate(
            ((momentum_hbm, momentum_ref), (grad_hbm, grad_ref), (q_hbm, q_ref), (weight_hbm, weight_ref))
        )
    ]
    for load in loads:
        load.start()
    for load in loads[:3]:
        load.wait()
    buffer = momentum_ref[...] + grad_ref[...].astype(jnp.float32)
    local = dot(buffer, q_ref[...], ((0,), (0,)))
    part[0:half] = local[:, 0:128].reshape(half, 8, 128)
    part[half:TILES] = local[:, 128:256].reshape(half, 8, 128)
    entered()

    def pass_on(k):
        for peer in relayed[k]:
            pl.semaphore_signal(relay.at[k], inc=1, device_id=peer, device_id_type=MESH_ID)

    def passed_on(k):
        pl.semaphore_wait(relay.at[k], len(relayed[k]))

    steps = [1 << k for k in range(8) if 1 << k < far]
    relayed = [others("zf", n_f, sorted({step, n_f - step})) for step in steps]
    if steps:
        pass_on(0)

    for i, d in enumerate(order):
        f = (f_me + d) % n_f
        for e in range(1, n_y):
            y = (y_me + e) % n_y
            remote(part.at[chunk(f, y)], got_y.at[i, e - 1], rs_send.at[0], rs_y.at[i], {"y": y})
    for k in range(1, len(steps)):
        passed_on(k - 1)
        pass_on(k)

    def after_y(i):
        drain(got_y.at[i], rs_y.at[i])
        total = part[chunk((f_me + order[i]) % n_f, y_me)]
        for e in range(1, n_y):
            total = total + got_y[i, e - 1]
        sum_y[i] = total
        for e in range(1, n_n):
            n = (n_me + e) % n_n
            share = sum_y.at[i, pl.ds(n * unit, unit)]
            remote(share, got_n.at[i, e - 1], rs_send.at[1], rs_n.at[i], {"zn": n})

    def after_n(i):
        drain(got_n.at[i], rs_n.at[i])
        total = sum_y[i, pl.ds(n_me * unit, unit)]
        for e in range(1, n_n):
            total = total + got_n[i, e - 1]
        sum_n[i] = total
        d = order[i]
        if d:
            remote(sum_n.at[i], got_f.at[i], rs_send.at[2], rs_f, {"zf": (f_me + d) % n_f})

    waiting = list(range(n_f))
    for i in range(min(n_f, 6)):
        after_y(waiting.pop(0))
    if steps:
        passed_on(len(steps) - 1)
    for i in range(n_f):
        if i >= 3 and waiting:
            after_y(waiting.pop(0))
        after_n(i)
    total = sum_n[n_f - 1]
    drain(got_f, rs_f)
    for i in range(n_f - 1):
        total = total + got_f[i]

    own = full.at[tile(f_me, n_me, y_me)]
    own[...] = total
    for n in range(n_n):
        peer = {"zf": (f_me + far) % n_f, "zn": (n_me + n) % n_n}
        remote(own, own, ag_send.at[0], ag_f.at[far], peer)
    for d in order[1:-1]:
        remote(own, own, ag_send.at[0], ag_f.at[d], {"zf": (f_me + d) % n_f})

    def spread_n(d):
        mine = full.at[tile((f_me - d + n_f) % n_f, n_me, y_me)]
        if d:
            drain(mine, ag_f.at[d])
        for e in range(1, n_n):
            remote(mine, mine, ag_send.at[1], ag_n.at[d], {"zn": (n_me + e) % n_n})

    def spread_y(d):
        mine = full.at[chunk((f_me - d + n_f) % n_f, y_me)]
        if d == far:
            drain(mine, ag_f.at[d])
        else:
            drain(full.at[0 : (n_n - 1) * unit], ag_n.at[d])
        for e in range(1, n_y):
            remote(mine, mine, ag_send.at[2], ag_y, {"y": (y_me + e) % n_y})

    near = order[:0:-1]
    lag = min(3, n_f - 1)
    for i in range(n_f - 1 + lag):
        if i < n_f - 1:
            spread_n(near[i])
        if i == n_f:
            spread_y(far)
        if i >= lag:
            spread_y(near[i - lag])
    if n_f - 1 + lag <= n_f:
        spread_y(far)
    drain(full.at[0 : TILES // n_y * (n_y - 1)], ag_y)

    whole = jnp.concatenate(
        [full[0:half].reshape(half * 8, 128), full[half:TILES].reshape(half * 8, 128)], axis=1
    )
    gram = dot(whole[:, 0:128], whole, ((0,), (0,)))
    first_part[0:16] = gram[:, 0:128].reshape(16, 8, 128)
    first_part[16:32] = gram[:, 128:256].reshape(16, 8, 128)
    first_scatter, first_gather, first_finish = sum_over(
        "fsdp", n_fsdp, first_part, first_got, first_total, FIRST_TILES // n_fsdp, first_sem
    )
    second_scatter, second_gather, second_finish = sum_over(
        "fsdp", n_fsdp, second_part, second_got, second_total, SECOND_TILES // n_fsdp, second_sem
    )
    cross_scatter, cross_gather, cross_finish = sum_over(
        "fsdp", n_fsdp, cross_part, cross_got, cross_total, CROSS_TILES // n_fsdp, cross_sem
    )
    first_scatter()
    second_part[...] = dot(whole[:, 128:256], whole[:, 128:256], ((0,), (0,))).reshape(16, 8, 128)
    cross = dot(buffer, whole, ((1,), (0,)))
    cross_part[0:14] = cross[:, 0:128].reshape(14, 8, 128)
    cross_part[14:28] = cross[:, 128:256].reshape(14, 8, 128)
    cross_part[28:32] = jnp.zeros((4, 8, 128), jnp.float32)
    first_gather()
    second_scatter()
    first_finish()
    second_gather()
    cross_scatter()

    eye = (
        lax.broadcasted_iota(jnp.int32, (128, 128), 0) == lax.broadcasted_iota(jnp.int32, (128, 128), 1)
    ).astype(jnp.float32)
    m[:, 0:128] = first_total[0:16].reshape(128, 128)
    m[:, 128:256] = first_total[16:32].reshape(128, 128)
    m[:, 256:384] = eye
    eliminate(m)
    second_finish()
    cross_gather()
    across, first = m[:, 128:256], m[:, 256:384]
    m[:, 0:128] = second_total[...].reshape(128, 128) - dot(across, across, ((0,), (0,)))
    m[:, 128:256] = -dot(across, first, ((0,), (0,)))
    m[:, 256:384] = eye
    eliminate(m)
    inverse = jnp.concatenate(
        [jnp.concatenate([first, jnp.zeros_like(first)], axis=1), m[:, 128:384]], axis=0
    )
    cross_finish()
    cross = jnp.concatenate(
        [cross_total[0:14].reshape(112, 128), cross_total[14:28].reshape(112, 128)], axis=1
    )
    right_factor = dot(cross, inverse, ((1,), (1,)))

    value = jnp.sum(right_factor * right_factor, axis=0, keepdims=True)
    square[0] = value
    for d in range(1, n_y):
        remote(square.at[0], square_y.at[d - 1], square_sem.at[0], square_sem.at[1], {"y": (y_me + d) % n_y})
    ortho = dot(whole, inverse, ((1,), (1,)))
    drain(square_y, square_sem.at[1])
    for d in range(1, n_y):
        value = value + square_y[d - 1]
    square[1] = value
    n_z = n_f * n_n
    z_me = f_me * n_n + n_me
    for d in far_first(n_z)[:-1]:
        z = (z_me + d) % n_z
        peer = {"zf": z // n_n, "zn": z % n_n}
        remote(square.at[1], square_z.at[d - 1], square_sem.at[2], square_sem.at[3], peer)
    new_momentum_ref[...] = buffer - (1.0 - momentum_decay) * dot(right_factor, ortho, ((1,), (1,)))

    drain(part.at[0 : TILES // n_y * (n_y - 1)], rs_send.at[0])
    drain(got_n, rs_send.at[1])
    drain(got_f, rs_send.at[2])
    drain(full.at[0 : (n_f - 2 + n_n) * unit], ag_send.at[0])
    drain(full.at[0 : (n_f - 1) * (n_n - 1) * unit], ag_send.at[1])
    drain(full.at[0 : TILES // n_y * (n_y - 1)], ag_send.at[2])
    drain(square_y, square_sem.at[0])
    drain(square_z, square_sem.at[3])
    drain(square_z, square_sem.at[2])
    loads[3].wait()
    for d in range(1, n_z):
        value = value + square_z[d - 1]
    q_new = right_factor / (jnp.sqrt(value) + norm_eps)
    new_q_ref[...] = q_new
    update = dot(q_new, ortho, ((1,), (1,)))
    new_weight_ref[...] = (weight_ref[...].astype(jnp.float32) - factor * update).astype(jnp.bfloat16)


def store_kernel(*refs):
    values, outs, sem = refs[:3], refs[3:6], refs[6]
    copies = [pltpu.make_async_copy(v, o, sem.at[i]) for i, (v, o) in enumerate(zip(values, outs))]
    for copy in copies:
        copy.start()
    for copy in copies:
        copy.wait()


def per_device(sizes, factor, weight, momentum, grad, q_prev):
    n_fsdp, n_f, n_n, n_y = sizes
    unit = TILES // (n_f * n_n * n_y)
    vmem = pl.BlockSpec(memory_space=pltpu.VMEM)
    hbm = pl.BlockSpec(memory_space=pltpu.HBM)
    dma = pltpu.SemaphoreType.DMA

    def tiles(*shape):
        return pltpu.VMEM((*shape, 8, 128), jnp.float32)

    def row(*shape):
        return pltpu.VMEM((*shape, 1, 256), jnp.float32)

    outs = (
        jax.ShapeDtypeStruct(weight.shape, jnp.bfloat16),
        jax.ShapeDtypeStruct(momentum.shape, jnp.float32),
        jax.ShapeDtypeStruct(q_prev.shape, jnp.float32),
    )
    results = pl.pallas_call(
        functools.partial(step_kernel, sizes, factor),
        out_shape=outs,
        in_specs=[hbm] * 4,
        out_specs=(vmem,) * 3,
        scratch_shapes=[
            pltpu.VMEM(weight.shape, weight.dtype),
            pltpu.VMEM(momentum.shape, momentum.dtype),
            pltpu.VMEM(grad.shape, grad.dtype),
            pltpu.VMEM(q_prev.shape, q_prev.dtype),
            tiles(TILES),
            tiles(TILES),
            tiles(n_f, n_y - 1, n_n * unit),
            tiles(n_f, n_n - 1, unit),
            tiles(n_f, n_n * unit),
            tiles(n_f, unit),
            tiles(n_f - 1, unit),
            tiles(FIRST_TILES),
            tiles(n_fsdp - 1, FIRST_TILES // n_fsdp),
            tiles(FIRST_TILES),
            tiles(SECOND_TILES),
            tiles(n_fsdp - 1, SECOND_TILES // n_fsdp),
            tiles(SECOND_TILES),
            tiles(CROSS_TILES),
            tiles(n_fsdp - 1, CROSS_TILES // n_fsdp),
            tiles(CROSS_TILES),
            pltpu.VMEM((128, 384), jnp.float32),
            row(2),
            row(n_y - 1),
            row(n_f * n_n - 1),
            dma((3,)),
            dma((n_f,)),
            dma((n_f,)),
            dma,
            dma((3,)),
            dma,
            dma((n_f,)),
            dma((n_f,)),
            dma((4,)),
            dma((4,)),
            dma((4,)),
            dma((4,)),
            dma((4,)),
            pltpu.SemaphoreType.REGULAR((2,)),
        ],
        compiler_params=pltpu.CompilerParams(
            collective_id=0, has_side_effects=True, vmem_limit_bytes=24 << 20
        ),
        name="step",
    )(*(pltpu.with_memory_space_constraint(x, pltpu.HBM) for x in (weight, momentum, grad, q_prev)))
    return pl.pallas_call(
        store_kernel,
        out_shape=outs,
        in_specs=[vmem] * 3,
        out_specs=(hbm,) * 3,
        scratch_shapes=[dma((3,))],
        compiler_params=pltpu.CompilerParams(vmem_limit_bytes=4 << 20),
        name="store",
    )(*results)


def split_tensor(n):
    return (8, 4, 4) if n == 128 else (n // 4, 2, 2)


def solution(mesh):
    n_fsdp, n_tensor = mesh.shape["fsdp"], mesh.shape["tensor"]
    sizes = (n_fsdp, *split_tensor(n_tensor))
    torus = Mesh(mesh.devices.reshape(sizes), ("fsdp", *TENSOR))
    factor = step_rate * math.sqrt(14336 / 4096)
    return jax.shard_map(
        functools.partial(per_device, sizes, factor),
        mesh=torus,
        in_specs=(P(TENSOR, "fsdp"), P(TENSOR, "fsdp"), P(TENSOR, "fsdp"), P(TENSOR, None)),
        out_specs=(P(TENSOR, "fsdp"), P(TENSOR, "fsdp"), P(TENSOR, None)),
        check_vma=False,
    )
```
